512 devices in a mesh: win: 128 (over y, z, core), head: 4 (over x).
Axes of the slice: x: 4, y: 8, z: 8, core: 2. Of those that a mesh axis runs over, the one named last changes fastest.
Arguments:
- tokens: bfloat16 [16384, 2560], P('win', 'head'), may hold values from -6 to 6
- queries: bfloat16 [16384, 1536], P('win', 'head'), may hold values from -64 to 64, as said below
- key_weight: bfloat16 [2560, 1536], P(None, 'head'), may hold values from -0.125 to 0.125
- value_weight: bfloat16 [2560, 1536], P(None, 'head'), may hold values from -0.125 to 0.125
- grad_out: bfloat16 [16384, 1536], P('win', 'head'), may hold values from -6 to 6
- owner_table: int32 [128, 64], replicated, may hold values from 0 to 127, as said below
- window_table: int32 [128, 64], replicated, may hold values from 0 to 16511, as said below
Outputs:
- attended: bfloat16 [16384, 1536], P('win', 'head')
- grad_queries: bfloat16 [16384, 1536], P('win', 'head')
- grad_tokens: bfloat16 [16384, 2560], P('win', 'head')
The draws below stay inside these ranges and needn't reach their ends.
Inputs may be any that keep to these rules, and one draw needn't show every extreme that they name: `owner_table`: the 64 groups of one window group go to distinct owners; in every draw some owner receives a group from every window group. `window_table`: groups with the same window number have the same owner. `queries`: rows may have scales far from one.
All inputs are finite; a program needn't handle non-finite values.
Results may differ from the reference program's by a relative error of at most 0.025.
The reference program's roundings to bfloat16 on the way (of `weights_low` and `grad_s_low`) count: a program that leaves them out, or rounds other values in their place, can miss the bound.
Values may be sent and summed in bfloat16 or wider, within the bound.
No kernel may reach another device: no remote copies, remote signals or barrier semaphores. Data moves between devices by JAX's collectives and lax.ppermute only.
A program may use at most 64 MiB of HBM per device.

```python
import math
import jax
import jax.numpy as jnp
from jax import lax

D = 2560
HEADS = 12
HD = 128
TOKENS = 16384
SOURCES = 128
PICKS = 64
GROUP = 2


def routing_tables(key):
    base = jax.random.fold_in(key, 7)
    first, second, third, fourth, fifth = jax.random.split(base, 5)
    owners = jnp.arange(SOURCES, dtype=jnp.int32)
    appeal = jax.random.randint(first, (SOURCES,), 0, 4)
    star = jax.random.randint(second, (), 0, SOURCES)
    appeal = jnp.where(owners == star, 1000, appeal)
    noise = jax.random.randint(third, (SOURCES, SOURCES), 0, 6)
    score = (appeal[None, :] + noise) * SOURCES + owners[None, :]
    chosen = lax.top_k(score, PICKS)[1].astype(jnp.int32)
    order_key = jax.random.randint(fourth, (SOURCES, PICKS), 0, 1 << 20) * PICKS + jnp.arange(PICKS, dtype=jnp.int32)[None, :]
    order = jnp.argsort(order_key, axis=1, stable=True)
    owner_table = jnp.take_along_axis(chosen, order, axis=1).astype(jnp.int32)
    sent_here = owner_table[None, :, :] == owners[:, None, None]
    filled = jnp.any(sent_here, axis=2)
    cuts = (jax.random.randint(fifth, (SOURCES, SOURCES), 0, 16) == 0) & filled
    segment = jnp.cumsum(cuts.astype(jnp.int32), axis=1)
    slot_ident = owners[:, None] * (SOURCES + 1) + segment
    window_table = slot_ident[owner_table, owners[:, None]].astype(jnp.int32)
    return (owner_table, window_table)


def draw_owner_table(key, part):
    return routing_tables(key)[0]


def draw_window_table(key, part):
    return routing_tables(key)[1]


def draw_queries(key, part):
    first = jax.random.fold_in(jax.random.fold_in(key, 11), 0)
    values = jax.random.normal(first, (TOKENS, HEADS * HD), jnp.float32)
    return jnp.clip(values, -6.0, 6.0).astype(jnp.bfloat16)


def levels(rng, shape, shards, low, largest):
    def one(axis_at, shards_of):
        steps = jax.random.uniform(jax.random.fold_in(jax.random.fold_in(rng, 6), axis_at), (shards_of,), jnp.float32, low / len(shards), largest / len(shards))
        return jnp.repeat(jnp.exp(steps), shape[axis_at] // shards_of).reshape((-1,) + (1,) * (len(shape) - axis_at - 1))

    gain = one(*shards[0])
    for cut in shards[1:]:
        gain = gain * one(*cut)
    return gain


def normal_values(own_key, extent, scale, most, cuts=(), kind=jnp.bfloat16):
    values = jax.random.normal(own_key, extent, jnp.float32) * scale
    if len(cuts) > 0:
        values = levels(own_key, extent, cuts, -0.22, 0.18) * values
    return jnp.clip(values, min=-most, max=most).astype(kind)


def setup_inputs(seed: int = 0) -> dict:
    splits = jax.random.split(jax.random.key(seed), 8)
    tokens = normal_values(splits[0], (TOKENS, D), 1.0, 6.0, ((0, 128), (1, 4)))
    queries = draw_queries(jax.random.fold_in(splits[7], 71), 0)
    key_weight = normal_values(splits[2], (D, HEADS * HD), D ** -0.5, 0.125, ((1, 4),))
    value_weight = normal_values(splits[3], (D, HEADS * HD), D ** -0.5, 0.125, ((1, 4),))
    grad_out = normal_values(splits[4], (TOKENS, HEADS * HD), 1.0, 6.0, ((0, 128), (1, 4)))
    owner_table = draw_owner_table(jax.random.fold_in(splits[7], 71), 0)
    window_table = draw_window_table(jax.random.fold_in(splits[7], 71), 0)
    return dict(tokens=tokens, queries=queries, key_weight=key_weight, value_weight=value_weight, grad_out=grad_out, owner_table=owner_table, window_table=window_table)


def rounded(value):
    return lax.optimization_barrier(value.astype(jnp.bfloat16)).astype(jnp.float32)

def attend(query, key, value, dout, same_window):
    scale = 1.0 / math.sqrt(HD)
    high = lax.Precision.HIGHEST
    scores = jnp.einsum('qhd,khd->hqk', query, key, precision=high) * scale
    scores = jnp.where(same_window[None], scores, -1e+30)
    top = lax.optimization_barrier(jnp.max(scores, axis=-1, keepdims=True))
    expd = jnp.exp(scores - top)
    weights = expd / lax.optimization_barrier(jnp.sum(expd, axis=-1, keepdims=True))
    weights_low = rounded(weights)
    output = rounded(jnp.einsum('hqk,khd->qhd', weights_low, value, precision=high))
    grad_v = jnp.einsum('hqk,qhd->khd', weights_low, dout, precision=high)
    grad_p = jnp.einsum('qhd,khd->hqk', dout, value, precision=high)
    delta = jnp.einsum('qhd,qhd->hq', dout, output, precision=high)
    grad_s = weights * (grad_p - delta[:, :, None])
    grad_s_low = rounded(grad_s)
    grad_q = jnp.einsum('hqk,khd->qhd', grad_s_low, key, precision=high) * scale
    grad_k = jnp.einsum('hqk,qhd->khd', grad_s_low, query, precision=high) * scale
    return (output.astype(jnp.bfloat16), grad_q.astype(jnp.bfloat16), grad_k.astype(jnp.bfloat16), grad_v.astype(jnp.bfloat16))

def reference(tokens, queries, key_weight, value_weight, grad_out, owner_table, window_table):
    count = SOURCES
    pick_count = PICKS
    group_rows = GROUP
    slot_count = count * group_rows
    width = HEADS * HD
    keys = jnp.dot(tokens, key_weight, preferred_element_type=jnp.float32).astype(jnp.bfloat16)
    values = jnp.dot(tokens, value_weight, preferred_element_type=jnp.float32).astype(jnp.bfloat16)
    owners = jnp.arange(count, dtype=jnp.int32)
    sent_here = owner_table[None, :, :] == owners[:, None, None]
    filled = jnp.any(sent_here, axis=2)
    positions = lax.optimization_barrier(jnp.sum(jnp.where(sent_here, jnp.arange(pick_count, dtype=jnp.int32)[None, None, :], 0), axis=2)).astype(jnp.int32)
    slot_windows = lax.optimization_barrier(jnp.sum(jnp.where(sent_here, window_table[None, :, :], 0), axis=2)).astype(jnp.int32)
    slot_windows = jnp.where(filled, slot_windows, -(owners[None, :] + 1)).astype(jnp.int32)
    token_windows = jnp.repeat(slot_windows, group_rows, axis=1)
    index = (owners[None, :, None] * pick_count + positions[:, :, None]) * group_rows
    index = (index + jnp.arange(group_rows, dtype=jnp.int32)[None, None, :]).reshape(count, slot_count).astype(jnp.int32)
    fill_rows = jnp.repeat(filled, group_rows, axis=1)

    def per_owner(owner):
        rows = index[owner]
        keep = fill_rows[owner][:, None]

        def take(array):
            picked = jnp.where(keep, array[rows].astype(jnp.float32), 0.0)
            return picked.reshape(slot_count, HEADS, HD)
        same_window = token_windows[owner][:, None] == token_windows[owner][None, :]
        results = attend(take(queries), take(keys), take(values), take(grad_out), same_window)
        return tuple((item.reshape(slot_count, width) for item in results))
    outputs = lax.map(per_owner, owners)

    def back(slot_rows):
        shaped = slot_rows.reshape(count, count, group_rows, width)
        picked = shaped[owner_table, owners[:, None]]
        return picked.reshape(count * pick_count * group_rows, width)
    attended = back(outputs[0])
    grad_queries = back(outputs[1])
    grad_keys = back(outputs[2])
    grad_values = back(outputs[3])
    grad_tokens = jnp.dot(grad_keys, key_weight.T, preferred_element_type=jnp.float32)
    grad_tokens = grad_tokens + jnp.dot(grad_values, value_weight.T, preferred_element_type=jnp.float32)
    return (attended, grad_queries, grad_tokens.astype(jnp.bfloat16))
```

```python
import math

import jax
import jax.numpy as jnp
from jax import lax
from jax.experimental import pallas as pl
from jax.experimental.pallas import tpu as pltpu
from jax.sharding import PartitionSpec as P

HD = 128
KINDS = 4
F32 = jnp.float32
BF16 = jnp.bfloat16
NN = (((1,), (0,)), ((), ()))
NT = (((1,), (1,)), ((), ()))
TN = (((0,), (0,)), ((), ()))


def dot(a, b, dims=NN):
    return lax.dot_general(a, b, dims, preferred_element_type=F32)


def iota(shape, dim):
    return lax.broadcasted_iota(jnp.int32, shape, dim)


def own_owners(owner_ref, group_rows, along):
    picks = owner_ref.shape[1]
    own = owner_ref[pl.ds(lax.axis_index("win"), 1), :]
    own = jnp.broadcast_to(own.astype(F32), (8, picks)).astype(BF16)
    tok = picks * group_rows
    if along == 1:
        spread = iota((picks, tok), 1) // group_rows == iota((picks, tok), 0)
        return dot(own, spread.astype(F32).astype(BF16))[0:1, :].astype(jnp.int32)
    spread = iota((tok, picks), 0) // group_rows == iota((tok, picks), 1)
    return dot(spread.astype(F32).astype(BF16), own, NT)[:, 0:1].astype(jnp.int32)


def targets(owner_ref, group_rows, along):
    own = own_owners(owner_ref, group_rows, along)
    inner = iota(own.shape, along) % group_rows
    parts = [own * (KINDS * group_rows) + kind * group_rows + inner for kind in range(KINDS)]
    return jnp.concatenate(parts, axis=along)


def send_body(group_rows, tok_ref, wk_ref, wv_ref, q_ref, do_ref, owner_ref, out_ref):
    piece = tok_ref[...]
    key = dot(piece, wk_ref[...]).astype(BF16)
    value = dot(piece, wv_ref[...]).astype(BF16)
    rows = jnp.concatenate([q_ref[...], do_ref[...], key, value], axis=0)
    target = targets(owner_ref, group_rows, 1)
    shape = (out_ref.shape[0], rows.shape[0])
    select = (iota(shape, 0) == target).astype(F32).astype(BF16)
    out_ref[...] = dot(select, rows).astype(BF16)


def order_matrix(block, group_rows, transposed):
    inner = KINDS * group_rows
    sources = block // inner
    a, b = iota((block, block), 0), iota((block, block), 1)
    if transposed:
        a, b = b, a
    match = (a % sources == b // inner) & (a // sources == b % inner)
    return match.astype(F32).astype(BF16)


def attend_body(group_rows, in_ref, owner_ref, window_ref, out_ref, q_s, do_s, k_s, v_s, o_s, dq_s, dk_s, dv_s):
    devices = owner_ref.shape[0]
    inner = KINDS * group_rows
    slots, width = q_s.shape
    block = 16 * inner
    scale = 1.0 / math.sqrt(HD)
    order = order_matrix(block, group_rows, False)
    ins = (q_s, do_s, k_s, v_s)
    for b in range(devices // 16):
        part = dot(order, in_ref[b * block : (b + 1) * block, :]).astype(BF16)
        for kind in range(KINDS):
            for r in range(group_rows):
                at = (kind * group_rows + r) * 16
                ins[kind][r * devices + b * 16 : r * devices + (b + 1) * 16, :] = part[at : at + 16, :]

    sent_here = owner_ref[...] == lax.axis_index("win")
    filled = jnp.max(sent_here.astype(F32), axis=1, keepdims=True)
    window = jnp.sum(jnp.where(sent_here, window_ref[...], 0).astype(F32), axis=1, keepdims=True)
    window = jnp.where(filled > 0, window, -(iota((devices, 1), 0) + 1).astype(F32))
    wide = jnp.broadcast_to(window, (devices, devices))
    same = wide == jnp.transpose(wide)
    same = jnp.where(same, 0.0, 1.0)
    other = jnp.concatenate([jnp.concatenate([same] * group_rows, axis=1)] * group_rows, axis=0) > 0

    for h in range(width // HD):
        cols = slice(h * HD, (h + 1) * HD)
        query, dout, key, value = q_s[:, cols], do_s[:, cols], k_s[:, cols], v_s[:, cols]
        scores = jnp.where(other, -1e30, dot(query, key, NT) * scale)
        top = jnp.max(scores, axis=1, keepdims=True)
        expd = jnp.exp(scores - top)
        weights = expd / jnp.sum(expd, axis=1, keepdims=True)
        weights_low = weights.astype(BF16)
        output = dot(weights_low, value).astype(BF16)
        o_s[:, cols] = output
        dv_s[:, cols] = dot(weights_low, dout, TN).astype(BF16)
        grad_p = dot(dout, value, NT)
        delta = jnp.sum(dout.astype(F32) * output.astype(F32), axis=1, keepdims=True)
        grad_s_low = (weights * (grad_p - delta)).astype(BF16)
        dq_s[:, cols] = (dot(grad_s_low, key) * scale).astype(BF16)
        dk_s[:, cols] = (dot(grad_s_low, query, TN) * scale).astype(BF16)

    back = order_matrix(block, group_rows, True)
    outs = (o_s, dq_s, dk_s, dv_s)
    for b in range(devices // 16):
        part = jnp.concatenate(
            [
                outs[kind][r * devices + b * 16 : r * devices + (b + 1) * 16, :]
                for kind in range(KINDS)
                for r in range(group_rows)
            ],
            axis=0,
        )
        out_ref[b * block : (b + 1) * block, :] = dot(back, part).astype(BF16)


def take_body(group_rows, in_ref, owner_ref, wk_ref, wv_ref, o_ref, dq_ref, term_ref):
    tok = o_ref.shape[0]
    target = targets(owner_ref, group_rows, 0)
    shape = (KINDS * tok, in_ref.shape[0])
    select = (iota(shape, 1) == target).astype(F32).astype(BF16)
    rows = dot(select, in_ref[...]).astype(BF16)
    o_ref[...] = rows[0:tok, :]
    dq_ref[...] = rows[tok : 2 * tok, :]
    dk, dv = rows[2 * tok : 3 * tok, :], rows[3 * tok : 4 * tok, :]
    parts, _, columns = term_ref.shape
    for p in range(parts):
        at = slice(p * columns, (p + 1) * columns)
        term = dot(dk, wk_ref[at, :], NT) + dot(dv, wv_ref[at, :], NT)
        term_ref[p] = term.astype(BF16)


def local(tokens, queries, key_weight, value_weight, grad_out, owner_table, window_table):
    devices = lax.axis_size("win")
    heads = lax.axis_size("head")
    tok, columns = tokens.shape
    width = queries.shape[1]
    group_rows = tok // owner_table.shape[1]
    packed = devices * KINDS * group_rows
    slots = devices * group_rows
    params = pltpu.CompilerParams(vmem_limit_bytes=32 * 1024 * 1024)

    def call(body, outs, scratch=(), flops=1, moved=1):
        return pl.pallas_call(
            body,
            out_shape=outs,
            scratch_shapes=list(scratch),
            compiler_params=params,
            cost_estimate=pl.CostEstimate(flops=flops, bytes_accessed=moved, transcendentals=0),
        )

    def exchange(rows):
        rows = rows.reshape(devices, KINDS * group_rows, width)
        rows = lax.all_to_all(rows, "win", split_axis=0, concat_axis=0, tiled=True)
        return rows.reshape(packed, width)

    piece = lax.all_gather(tokens, "head", axis=1, tiled=True)
    sent = call(
        lambda *refs: send_body(group_rows, *refs),
        jax.ShapeDtypeStruct((packed, width), BF16),
    )(piece, key_weight, value_weight, queries, grad_out, owner_table)
    arrived = exchange(sent)
    results = call(
        lambda *refs: attend_body(group_rows, *refs),
        jax.ShapeDtypeStruct((packed, width), BF16),
        [pltpu.VMEM((slots, width), BF16)] * 8,
    )(arrived, owner_table, window_table)
    returned = exchange(results)
    attended, grad_queries, term = call(
        lambda *refs: take_body(group_rows, *refs),
        (
            jax.ShapeDtypeStruct((tok, width), BF16),
            jax.ShapeDtypeStruct((tok, width), BF16),
            jax.ShapeDtypeStruct((heads, tok, columns), BF16),
        ),
    )(returned, owner_table, key_weight, value_weight)
    terms = lax.all_to_all(term, "head", split_axis=0, concat_axis=0, tiled=True)
    grad_tokens = jnp.sum(terms.astype(F32), axis=0).astype(BF16)
    return (attended, grad_queries, grad_tokens)


def solution(mesh):
    in_specs = (
        P("win", "head"),
        P("win", "head"),
        P(None, "head"),
        P(None, "head"),
        P("win", "head"),
        P(),
        P(),
    )
    out_specs = (P("win", "head"), P("win", "head"), P("win", "head"))
    return jax.shard_map(local, mesh=mesh, in_specs=in_specs, out_specs=out_specs, check_vma=False)
```

```python
import math

import jax
import jax.numpy as jnp
from jax import lax
from jax.experimental import pallas as pl
from jax.experimental.pallas import tpu as pltpu
from jax.sharding import PartitionSpec as P

HD = 128
KINDS = 4
F32 = jnp.float32
BF16 = jnp.bfloat16
NN = (((1,), (0,)), ((), ()))
NT = (((1,), (1,)), ((), ()))
TN = (((0,), (0,)), ((), ()))


def dot(a, b, dims=NN):
    return lax.dot_general(a, b, dims, preferred_element_type=F32)


def iota(shape, dim):
    return lax.broadcasted_iota(jnp.int32, shape, dim)


def targets(owner_ref, group_rows):
    picks, devices = owner_ref.shape
    tok = picks * group_rows
    here = iota((picks, devices), 1) == lax.axis_index("win")
    own = jnp.sum(jnp.where(here, owner_ref[...], 0).astype(F32), axis=1, keepdims=True)
    spread = iota((picks, tok), 1) // group_rows == iota((picks, tok), 0)
    own = jnp.sum(jnp.where(spread, own, 0.0), axis=0, keepdims=True)
    inner = (iota((1, tok), 1) % group_rows).astype(F32)
    return own * (KINDS * group_rows) + inner


def start_weights(wk_hbm, wv_hbm, wk_s, wv_s, sems, chunks):
    rows = wk_s.shape[0] // chunks
    copies = []
    for c in range(chunks):
        at = pl.ds(c * rows, rows)
        pair = (
            pltpu.make_async_copy(wk_hbm.at[at], wk_s.at[at], sems.at[2 * c]),
            pltpu.make_async_copy(wv_hbm.at[at], wv_s.at[at], sems.at[2 * c + 1]),
        )
        pair[0].start()
        pair[1].start()
        copies.append(pair)
    return copies


def send_body(
    group_rows,
    tok_ref,
    owner_hbm,
    q_hbm,
    do_hbm,
    wk_hbm,
    wv_hbm,
    out_ref,
    owner_s,
    rows_s,
    wk_s,
    wv_s,
    sems,
):
    tok = tok_ref.shape[0]
    chunks = (sems.shape[0] - 3) // 2
    copy_owner = pltpu.make_async_copy(owner_hbm, owner_s, sems.at[2 * chunks + 2])
    copy_owner.start()
    copies = start_weights(wk_hbm, wv_hbm, wk_s, wv_s, sems, chunks)
    copy_q = pltpu.make_async_copy(q_hbm, rows_s.at[pl.ds(0, tok)], sems.at[2 * chunks])
    copy_do = pltpu.make_async_copy(do_hbm, rows_s.at[pl.ds(tok, tok)], sems.at[2 * chunks + 1])
    copy_q.start()
    copy_do.start()
    copy_owner.wait()
    target = targets(owner_s, group_rows)
    target = jnp.concatenate([target + kind * group_rows for kind in range(KINDS)], axis=1)
    shape = (out_ref.shape[0], KINDS * tok)
    select = (iota(shape, 0) == target.astype(jnp.int32)).astype(F32).astype(BF16)
    rows = wk_s.shape[0] // chunks
    key = value = None
    for c, (copy_k, copy_v) in enumerate(copies):
        at = slice(c * rows, (c + 1) * rows)
        copy_k.wait()
        part = dot(tok_ref[:, at], wk_s[at, :])
        key = part if key is None else key + part
        copy_v.wait()
        part = dot(tok_ref[:, at], wv_s[at, :])
        value = part if value is None else value + part
    rows_s[2 * tok : 3 * tok, :] = key.astype(BF16)
    rows_s[3 * tok : 4 * tok, :] = value.astype(BF16)
    copy_q.wait()
    copy_do.wait()
    out_ref[...] = dot(select, rows_s[...]).astype(BF16)


def order_matrix(block, group_rows, transposed):
    inner = KINDS * group_rows
    sources = block // inner
    a, b = iota((block, block), 0), iota((block, block), 1)
    if transposed:
        a, b = b, a
    match = (a % sources == b // inner) & (a // sources == b % inner)
    return match.astype(F32).astype(BF16)


def attend_body(group_rows, in_ref, owner_ref, window_ref, out_ref, q_s, do_s, k_s, v_s, o_s, dq_s, dk_s, dv_s):
    devices = owner_ref.shape[1]
    inner = KINDS * group_rows
    slots, width = q_s.shape
    block = 16 * inner
    scale = 1.0 / math.sqrt(HD)
    order = order_matrix(block, group_rows, False)
    ins = (q_s, do_s, k_s, v_s)
    for b in range(devices // 16):
        part = dot(order, in_ref[b * block : (b + 1) * block, :]).astype(BF16)
        for kind in range(KINDS):
            for r in range(group_rows):
                at = (kind * group_rows + r) * 16
                ins[kind][r * devices + b * 16 : r * devices + (b + 1) * 16, :] = part[at : at + 16, :]

    sent_here = owner_ref[...] == lax.axis_index("win")
    filled = jnp.max(sent_here.astype(F32), axis=0, keepdims=True)
    window = jnp.sum(jnp.where(sent_here, window_ref[...], 0).astype(F32), axis=0, keepdims=True)
    window = jnp.where(filled > 0, window, -(iota((1, devices), 1) + 1).astype(F32))
    wide = jnp.broadcast_to(window, (devices, devices))
    same = wide == jnp.transpose(wide)
    same = jnp.where(same, 0.0, 1.0)
    other = jnp.concatenate([jnp.concatenate([same] * group_rows, axis=1)] * group_rows, axis=0) > 0

    for h in range(width // HD):
        cols = slice(h * HD, (h + 1) * HD)
        query, dout, key, value = q_s[:, cols], do_s[:, cols], k_s[:, cols], v_s[:, cols]
        scores = jnp.where(other, -1e30, dot(query, key, NT) * scale)
        top = jnp.max(scores, axis=1, keepdims=True)
        expd = jnp.exp(scores - top)
        weights = expd / jnp.sum(expd, axis=1, keepdims=True)
        weights_low = weights.astype(BF16)
        output = dot(weights_low, value).astype(BF16)
        o_s[:, cols] = output
        dv_s[:, cols] = dot(weights_low, dout, TN).astype(BF16)
        grad_p = dot(dout, value, NT)
        delta = jnp.sum(dout.astype(F32) * output.astype(F32), axis=1, keepdims=True)
        grad_s_low = (weights * (grad_p - delta)).astype(BF16)
        dq_s[:, cols] = (dot(grad_s_low, key) * scale).astype(BF16)
        dk_s[:, cols] = (dot(grad_s_low, query, TN) * scale).astype(BF16)

    back = order_matrix(block, group_rows, True)
    outs = (o_s, dq_s, dk_s, dv_s)
    for b in range(devices // 16):
        part = jnp.concatenate(
            [
                outs[kind][r * devices + b * 16 : r * devices + (b + 1) * 16, :]
                for kind in range(KINDS)
                for r in range(group_rows)
            ],
            axis=0,
        )
        out_ref[b * block : (b + 1) * block, :] = dot(back, part).astype(BF16)


def take_body(
    group_rows, in_ref, owner_ref, wk_ref, wv_ref, o_hbm, dq_hbm, term_ref, rows_s, sems
):
    parts, tok, columns = term_ref.shape
    target = targets(owner_ref, group_rows)
    target = jnp.transpose(jnp.broadcast_to(target, (tok, tok)))[:, 0:1]
    target = jnp.concatenate([target + kind * group_rows for kind in range(KINDS)], axis=0)
    shape = (KINDS * tok, in_ref.shape[0])
    select = (iota(shape, 1) == target.astype(jnp.int32)).astype(F32).astype(BF16)
    rows_s[...] = dot(select, in_ref[...]).astype(BF16)
    copy_o = pltpu.make_async_copy(rows_s.at[pl.ds(0, tok)], o_hbm, sems.at[0])
    copy_dq = pltpu.make_async_copy(rows_s.at[pl.ds(tok, tok)], dq_hbm, sems.at[1])
    copy_o.start()
    copy_dq.start()
    dk, dv = rows_s[2 * tok : 3 * tok, :], rows_s[3 * tok : 4 * tok, :]
    for p in range(parts):
        at = slice(p * columns, (p + 1) * columns)
        term = dot(dk, wk_ref[at, :], NT) + dot(dv, wv_ref[at, :], NT)
        term_ref[p] = term.astype(BF16)
    copy_o.wait()
    copy_dq.wait()


def local(tokens, queries, key_weight, value_weight, grad_out, owner_table, window_table):
    devices = lax.axis_size("win")
    heads = lax.axis_size("head")
    tok, columns = tokens.shape
    width = queries.shape[1]
    group_rows = tok // owner_table.shape[1]
    packed = devices * KINDS * group_rows
    slots = devices * group_rows

    vmem = pl.BlockSpec(memory_space=pltpu.VMEM)
    hbm = pl.BlockSpec(memory_space=pltpu.HBM)

    def call(body, outs, in_specs, out_specs, scratch):
        return pl.pallas_call(
            lambda *refs: body(group_rows, *refs),
            out_shape=outs,
            in_specs=in_specs,
            out_specs=out_specs,
            scratch_shapes=scratch,
            compiler_params=pltpu.CompilerParams(vmem_limit_bytes=32 << 20),
        )

    def exchange(rows):
        rows = rows.reshape(devices, KINDS * group_rows, width)
        rows = lax.all_to_all(rows, "win", split_axis=0, concat_axis=0, tiled=True)
        return rows.reshape(packed, width)

    owners, windows = owner_table.T, window_table.T
    packed_rows = jax.ShapeDtypeStruct((packed, width), BF16)
    token_rows = jax.ShapeDtypeStruct((tok, width), BF16)
    piece = lax.all_gather(tokens, "head", axis=1, tiled=True)
    stay = [
        pltpu.with_memory_space_constraint(array, pltpu.HBM)
        for array in (owners, queries, grad_out, key_weight, value_weight)
    ]
    sent = call(
        send_body,
        packed_rows,
        [vmem] + [hbm] * len(stay),
        vmem,
        [
            pltpu.VMEM(owners.shape, jnp.int32),
            pltpu.VMEM((KINDS * tok, width), BF16),
            pltpu.VMEM(key_weight.shape, BF16),
            pltpu.VMEM(key_weight.shape, BF16),
            pltpu.SemaphoreType.DMA((11,)),
        ],
    )(piece, *stay)
    arrived = exchange(sent)
    results = call(
        attend_body, packed_rows, [vmem] * 3, vmem, [pltpu.VMEM((slots, width), BF16)] * 8
    )(arrived, owners, windows)
    returned = exchange(results)
    attended, grad_queries, term = call(
        take_body,
        (token_rows, token_rows, jax.ShapeDtypeStruct((heads, tok, columns), BF16)),
        [vmem] * 4,
        (hbm, hbm, vmem),
        [pltpu.VMEM((KINDS * tok, width), BF16), pltpu.SemaphoreType.DMA((2,))],
    )(returned, owners, key_weight, value_weight)
    terms = lax.all_to_all(term, "head", split_axis=0, concat_axis=0, tiled=True)
    grad_tokens = jnp.sum(terms.astype(F32), axis=0).astype(BF16)
    return (attended, grad_queries, grad_tokens)


def solution(mesh):
    in_specs = (
        P("win", "head"),
        P("win", "head"),
        P(None, "head"),
        P(None, "head"),
        P("win", "head"),
        P(),
        P(),
    )
    out_specs = (P("win", "head"), P("win", "head"), P("win", "head"))
    return jax.shard_map(local, mesh=mesh, in_specs=in_specs, out_specs=out_specs, check_vma=False)
```

```python
import math

import jax
import jax.numpy as jnp
from jax import lax
from jax.experimental import pallas as pl
from jax.experimental.pallas import tpu as pltpu
from jax.sharding import PartitionSpec as P

HD = 128
KINDS = 4
F32 = jnp.float32
BF16 = jnp.bfloat16
NN = (((1,), (0,)), ((), ()))
NT = (((1,), (1,)), ((), ()))
TN = (((0,), (0,)), ((), ()))


def dot(a, b, dims=NN):
    return lax.dot_general(a, b, dims, preferred_element_type=F32)


def iota(shape, dim):
    return lax.broadcasted_iota(jnp.int32, shape, dim)


def targets(owner_ref, group_rows):
    picks, devices = owner_ref.shape
    tok = picks * group_rows
    here = iota((picks, devices), 1) == lax.axis_index("win")
    own = jnp.sum(jnp.where(here, owner_ref[...], 0).astype(F32), axis=1, keepdims=True)
    spread = iota((picks, tok), 1) // group_rows == iota((picks, tok), 0)
    own = jnp.sum(jnp.where(spread, own, 0.0), axis=0, keepdims=True)
    inner = (iota((1, tok), 1) % group_rows).astype(F32)
    return own * (KINDS * group_rows) + inner


def select_rows(owner_ref, group_rows, kinds, shape):
    target = targets(owner_ref, group_rows)
    target = jnp.concatenate([target + kind * group_rows for kind in kinds], axis=1)
    return (iota(shape, 0) == target.astype(jnp.int32)).astype(F32).astype(BF16)


def pack_body(group_rows, owner_hbm, q_hbm, do_hbm, pack_ref, owner_s, rows_s, sems):
    tok = q_hbm.shape[0]
    copy_owner = pltpu.make_async_copy(owner_hbm, owner_s, sems.at[0])
    copy_q = pltpu.make_async_copy(q_hbm, rows_s.at[pl.ds(0, tok)], sems.at[1])
    copy_do = pltpu.make_async_copy(do_hbm, rows_s.at[pl.ds(tok, tok)], sems.at[2])
    copy_owner.start()
    copy_q.start()
    copy_do.start()
    copy_owner.wait()
    select = select_rows(owner_s, group_rows, (0, 1), (pack_ref.shape[0], 2 * tok))
    copy_q.wait()
    copy_do.wait()
    pack_ref[...] = dot(select, rows_s[...]).astype(BF16)


def send_body(group_rows, tok_ref, pack_ref, owner_ref, wk_ref, wv_hbm, out_ref, wv_s, sem):
    parts, tok, columns = tok_ref.shape
    copy_v = pltpu.make_async_copy(wv_hbm, wv_s, sem)
    copy_v.start()
    select = select_rows(owner_ref, group_rows, (2, 3), (out_ref.shape[0], 2 * tok))

    def project(weight_ref):
        total = dot(tok_ref[0], weight_ref[0:columns, :])
        for p in range(1, parts):
            total = total + dot(tok_ref[p], weight_ref[p * columns : (p + 1) * columns, :])
        return total.astype(BF16)

    key = project(wk_ref)
    copy_v.wait()
    rows = jnp.concatenate([key, project(wv_s)], axis=0)
    out_ref[...] = (pack_ref[...].astype(F32) + dot(select, rows)).astype(BF16)


def order_matrix(block, group_rows, transposed):
    inner = KINDS * group_rows
    sources = block // inner
    a, b = iota((block, block), 0), iota((block, block), 1)
    if transposed:
        a, b = b, a
    match = (a % sources == b // inner) & (a // sources == b % inner)
    return match.astype(F32).astype(BF16)


def attend_body(group_rows, in_ref, owner_ref, window_ref, out_ref, q_s, do_s, k_s, v_s, o_s, dq_s, dk_s, dv_s):
    devices = owner_ref.shape[1]
    inner = KINDS * group_rows
    slots, width = q_s.shape
    block = 16 * inner
    scale = 1.0 / math.sqrt(HD)
    order = order_matrix(block, group_rows, False)
    ins = (q_s, do_s, k_s, v_s)
    for b in range(devices // 16):
        part = dot(order, in_ref[b * block : (b + 1) * block, :]).astype(BF16)
        for kind in range(KINDS):
            for r in range(group_rows):
                at = (kind * group_rows + r) * 16
                ins[kind][r * devices + b * 16 : r * devices + (b + 1) * 16, :] = part[at : at + 16, :]

    sent_here = owner_ref[...] == lax.axis_index("win")
    filled = jnp.max(sent_here.astype(F32), axis=0, keepdims=True)
    window = jnp.sum(jnp.where(sent_here, window_ref[...], 0).astype(F32), axis=0, keepdims=True)
    window = jnp.where(filled > 0, window, -(iota((1, devices), 1) + 1).astype(F32))
    wide = jnp.broadcast_to(window, (devices, devices))
    same = wide == jnp.transpose(wide)
    same = jnp.where(same, 0.0, 1.0)
    other = jnp.concatenate([jnp.concatenate([same] * group_rows, axis=1)] * group_rows, axis=0) > 0

    for h in range(width // HD):
        cols = slice(h * HD, (h + 1) * HD)
        query, dout, key, value = q_s[:, cols], do_s[:, cols], k_s[:, cols], v_s[:, cols]
        scores = jnp.where(other, -1e30, dot(query, key, NT) * scale)
        top = jnp.max(scores, axis=1, keepdims=True)
        expd = jnp.exp(scores - top)
        weights = expd / jnp.sum(expd, axis=1, keepdims=True)
        weights_low = weights.astype(BF16)
        output = dot(weights_low, value).astype(BF16)
        o_s[:, cols] = output
        dv_s[:, cols] = dot(weights_low, dout, TN).astype(BF16)
        grad_p = dot(dout, value, NT)
        delta = jnp.sum(dout.astype(F32) * output.astype(F32), axis=1, keepdims=True)
        grad_s_low = (weights * (grad_p - delta)).astype(BF16)
        dq_s[:, cols] = (dot(grad_s_low, key) * scale).astype(BF16)
        dk_s[:, cols] = (dot(grad_s_low, query, TN) * scale).astype(BF16)

    back = order_matrix(block, group_rows, True)
    outs = (o_s, dq_s, dk_s, dv_s)
    for b in range(devices // 16):
        part = jnp.concatenate(
            [
                outs[kind][r * devices + b * 16 : r * devices + (b + 1) * 16, :]
                for kind in range(KINDS)
                for r in range(group_rows)
            ],
            axis=0,
        )
        out_ref[b * block : (b + 1) * block, :] = dot(back, part).astype(BF16)


def taken(group_rows, in_ref, owner_ref, kinds):
    tok = owner_ref.shape[0] * group_rows
    target = targets(owner_ref, group_rows)
    target = jnp.transpose(jnp.broadcast_to(target, (tok, tok)))[:, 0:1]
    target = jnp.concatenate([target + kind * group_rows for kind in kinds], axis=0)
    shape = (len(kinds) * tok, in_ref.shape[0])
    select = (iota(shape, 1) == target.astype(jnp.int32)).astype(F32).astype(BF16)
    return dot(select, in_ref[...]).astype(BF16)


def term_body(group_rows, in_ref, owner_ref, wk_ref, wv_ref, term_ref):
    parts, tok, columns = term_ref.shape
    rows = taken(group_rows, in_ref, owner_ref, (2, 3))
    dk, dv = rows[:tok, :], rows[tok:, :]
    for p in range(parts):
        at = slice(p * columns, (p + 1) * columns)
        term = dot(dk, wk_ref[at, :], NT) + dot(dv, wv_ref[at, :], NT)
        term_ref[p] = term.astype(BF16)


def take_body(group_rows, in_ref, owner_ref, o_ref, dq_ref):
    tok = o_ref.shape[0]
    rows = taken(group_rows, in_ref, owner_ref, (0, 1))
    o_ref[...] = rows[:tok, :]
    dq_ref[...] = rows[tok:, :]


def local(tokens, queries, key_weight, value_weight, grad_out, owner_table, window_table):
    devices = lax.axis_size("win")
    heads = lax.axis_size("head")
    tok, columns = tokens.shape
    width = queries.shape[1]
    group_rows = tok // owner_table.shape[1]
    packed = devices * KINDS * group_rows
    slots = devices * group_rows

    vmem = pl.BlockSpec(memory_space=pltpu.VMEM)
    hbm = pl.BlockSpec(memory_space=pltpu.HBM)

    def call(body, outs, in_specs, out_specs, scratch):
        return pl.pallas_call(
            lambda *refs: body(group_rows, *refs),
            out_shape=outs,
            in_specs=in_specs,
            out_specs=out_specs,
            scratch_shapes=scratch,
            compiler_params=pltpu.CompilerParams(vmem_limit_bytes=32 << 20),
        )

    def exchange(rows):
        rows = rows.reshape(devices, KINDS * group_rows, width)
        rows = lax.all_to_all(rows, "win", split_axis=0, concat_axis=0, tiled=True)
        return rows.reshape(packed, width)

    owners, windows = owner_table.T, window_table.T
    packed_rows = jax.ShapeDtypeStruct((packed, width), BF16)
    token_rows = jax.ShapeDtypeStruct((tok, width), BF16)
    copies = jnp.broadcast_to(tokens[None], (heads, tok, columns))
    piece = lax.all_to_all(copies, "head", split_axis=0, concat_axis=0, tiled=True)
    owners_hbm, queries, grad_out, value_hbm = (
        pltpu.with_memory_space_constraint(array, pltpu.HBM)
        for array in (owners, queries, grad_out, value_weight)
    )
    pack = call(
        pack_body,
        packed_rows,
        [hbm] * 3,
        vmem,
        [
            pltpu.VMEM(owners.shape, jnp.int32),
            pltpu.VMEM((2 * tok, width), BF16),
            pltpu.SemaphoreType.DMA((3,)),
        ],
    )(owners_hbm, queries, grad_out)
    sent = call(
        send_body,
        packed_rows,
        [vmem] * 4 + [hbm],
        vmem,
        [pltpu.VMEM(value_weight.shape, BF16), pltpu.SemaphoreType.DMA],
    )(piece, pack, owners, key_weight, value_hbm)
    arrived = exchange(sent)
    results = call(
        attend_body, packed_rows, [vmem] * 3, vmem, [pltpu.VMEM((slots, width), BF16)] * 8
    )(arrived, owners, windows)
    returned = exchange(results)
    term = call(
        term_body, jax.ShapeDtypeStruct((heads, tok, columns), BF16), [vmem] * 4, vmem, []
    )(returned, owners, key_weight, value_weight)
    attended, grad_queries = call(
        take_body, (token_rows, token_rows), [vmem] * 2, (vmem, vmem), []
    )(returned, owners)
    terms = lax.all_to_all(term, "head", split_axis=0, concat_axis=0, tiled=True)
    grad_tokens = jnp.sum(terms.astype(F32), axis=0).astype(BF16)
    return (attended, grad_queries, grad_tokens)


def solution(mesh):
    in_specs = (
        P("win", "head"),
        P("win", "head"),
        P(None, "head"),
        P(None, "head"),
        P("win", "head"),
        P(),
        P(),
    )
    out_specs = (P("win", "head"), P("win", "head"), P("win", "head"))
    return jax.shard_map(local, mesh=mesh, in_specs=in_specs, out_specs=out_specs, check_vma=False)
```
